32 devices in a mesh: frames: 16 (over z, y, core), dp: 2 (over x).
Axes of the slice: x: 2, y: 2, z: 4, core: 2. Of those that a mesh axis runs over, the one named last changes fastest.
Arguments:
- shifted: bfloat16 [2, 64, 16, 16, 640], P('dp', 'frames'), may hold values from -6 to 6
- out_grad: bfloat16 [2, 64, 16, 16, 640], P('dp', 'frames'), may hold values from -6 to 6
- conv_weight: bfloat16 [640, 5760], P('frames'), may hold values from -0.078125 to 0.078125
- norm_gain: float32 [640], replicated, may hold values from 0.5 to 2
- norm_bias: float32 [640], replicated, may hold values from -4 to 4
- shift_fwd: int32 [80], replicated, may hold values from 0 to 639, as said below
- shift_bwd: int32 [80], replicated, may hold values from 0 to 639, as said below
Outputs:
- in_grad: bfloat16 [2, 64, 16, 16, 640], P('dp', 'frames')
- weight_grad: float32 [640, 5760], P('frames')
- gain_grad: float32 [640], replicated
- bias_grad: float32 [640], replicated
The draws below stay inside these ranges and needn't reach their ends.
Inputs may be any that keep to these rules, and one draw needn't show every extreme that they name: `shift_fwd`: 80 distinct channel numbers, none of them in shift_bwd. `shift_bwd`: 80 distinct channel numbers, none of them in shift_fwd.
All inputs are finite; a program needn't handle non-finite values.
Results may differ from the reference program's by a relative error of at most 0.003.
Values may be sent and summed in bfloat16 or wider, within the bound.
No kernel may reach another device: no remote copies, remote signals or barrier semaphores. Data moves between devices by JAX's collectives and lax.ppermute only.
A program may use at most 128 MiB of HBM per device.

```python
import math
import jax
import jax.numpy as jnp
from jax import lax

CH = 640
GROUP_CH = 20
TAPS = 9
FOLD = 80
ROWS = 16
COLS = 16
FRAMES = 64
VIDEOS = 2


def shift_channels(key):
    return jax.random.permutation(jax.random.fold_in(key, 17), CH).astype(jnp.int32)


def draw_shift_fwd(key, part):
    return shift_channels(key)[:FOLD]


def draw_shift_bwd(key, part):
    return shift_channels(key)[FOLD:2 * FOLD]


def steps_of(own_key, shape, cuts, low, top_value):
    def one(axis_at, blocks):
        steps = jax.random.uniform(jax.random.fold_in(jax.random.fold_in(own_key, 6), axis_at), (blocks,), jnp.float32, low / len(cuts), top_value / len(cuts))
        return jnp.repeat(jnp.exp(steps), shape[axis_at] // blocks).reshape((-1,) + (1,) * (len(shape) - axis_at - 1))

    factor_of = one(*cuts[0])
    for cut in cuts[1:]:
        factor_of = factor_of * one(*cut)
    return factor_of


def normal_values(own_key, shape, deviation, reach, split=(), kind=jnp.bfloat16):
    values = jax.random.normal(own_key, shape, jnp.float32) * deviation
    if len(split) > 0:
        values = steps_of(own_key, shape, split, -0.22, 0.18) * values
    return jnp.clip(values, min=-reach, max=reach).astype(kind)


def setup_inputs(seed: int = 0) -> dict:
    splits = jax.random.split(jax.random.key(seed), 8)
    return {
        "shifted": normal_values(splits[0], (VIDEOS, FRAMES, ROWS, COLS, CH), 1.0, 6.0, ((0, 2), (1, 16))),
        "out_grad": normal_values(splits[1], (VIDEOS, FRAMES, ROWS, COLS, CH), 1.0, 6.0, ((0, 2), (1, 16))),
        "conv_weight": normal_values(splits[2], (CH, TAPS * CH), (TAPS * CH) ** -0.5, 0.078125, ((0, 16),)),
        "norm_gain": jnp.clip(jnp.exp(jax.random.uniform(splits[3], (CH,), jnp.float32, math.log(0.5), math.log(2.0))), 0.5, 2.0),
        "norm_bias": normal_values(splits[4], (CH,), 1.0, 4.0, (), jnp.float32),
        "shift_fwd": draw_shift_fwd(jax.random.fold_in(splits[7], 71), 0),
        "shift_bwd": draw_shift_bwd(jax.random.fold_in(splits[7], 71), 0),
    }


epsilon = 1e-05

def pad_space(values):
    return jnp.pad(values, ((0, 0), (1, 1), (1, 1), (0, 0)))

def local_grads(shifted, out_grad, conv_weight, norm_gain, norm_bias):
    frame_count, row_count, col_count, channels = shifted.shape
    groups = channels // GROUP_CH
    values = shifted.astype(jnp.float32).reshape(frame_count, row_count * col_count, groups, GROUP_CH)
    center = lax.optimization_barrier(jnp.mean(values, axis=(1, 3), keepdims=True))
    spread = lax.optimization_barrier(jnp.mean(jnp.square(values - center), axis=(1, 3), keepdims=True))
    inverse = lax.rsqrt(spread + epsilon)
    grouped_normed = (values - center) * inverse
    normed = grouped_normed.reshape(frame_count, row_count, col_count, channels)
    before = normed * norm_gain + norm_bias
    activation = jax.nn.silu(before).astype(jnp.bfloat16)
    act_padded = pad_space(activation)
    grad_padded = pad_space(out_grad)
    grad_rows = out_grad.reshape(-1, channels)
    act_grad = jnp.zeros((grad_rows.shape[0], channels), jnp.float32)
    weight_parts = []
    for tap_index in range(9):
        row_off, col_off = divmod(tap_index, 3)
        grad_view = grad_padded[:, 2 - row_off:2 - row_off + row_count, 2 - col_off:2 - col_off + col_count, :].reshape(-1, channels)
        act_grad = act_grad + jnp.dot(grad_view, conv_weight[:, tap_index * channels:(tap_index + 1) * channels], preferred_element_type=jnp.float32)
        act_view = act_padded[:, row_off:row_off + row_count, col_off:col_off + col_count, :].reshape(-1, channels)
        weight_parts.append(lax.dot_general(grad_rows, act_view, (((0,), (0,)), ((), ())), preferred_element_type=jnp.float32))
    weight_grad = jnp.concatenate(weight_parts, axis=1)
    sigmoid_val = jax.nn.sigmoid(before)
    pre_grad = act_grad.reshape(before.shape) * sigmoid_val * (1.0 + before * (1.0 - sigmoid_val))
    gain_part = lax.optimization_barrier(jnp.sum(pre_grad * normed, axis=(0, 1, 2)))
    bias_part = lax.optimization_barrier(jnp.sum(pre_grad, axis=(0, 1, 2)))
    norm_grad = (pre_grad * norm_gain).reshape(values.shape)
    first_mean = lax.optimization_barrier(jnp.mean(norm_grad, axis=(1, 3), keepdims=True))
    second_mean = lax.optimization_barrier(jnp.mean(norm_grad * grouped_normed, axis=(1, 3), keepdims=True))
    shifted_grad = ((norm_grad - first_mean - grouped_normed * second_mean) * inverse).reshape(shifted.shape)
    return (shifted_grad.astype(jnp.bfloat16), weight_grad, gain_part, bias_part)

def reference(shifted, out_grad, conv_weight, norm_gain, norm_bias, shift_fwd, shift_bwd):
    scale = float(VIDEOS * FRAMES * ROWS * COLS) ** (-0.5)
    grads_list = []
    weight_total = jnp.zeros((CH, TAPS * CH), jnp.float32)
    gain_total = jnp.zeros((CH,), jnp.float32)
    bias_total = jnp.zeros((CH,), jnp.float32)
    for video in range(VIDEOS):
        shifted_grad, weight_part, gain_part, bias_part = local_grads(shifted[video], out_grad[video], conv_weight, norm_gain, norm_bias)
        grads_list.append(shifted_grad)
        weight_total = weight_total + weight_part
        gain_total = gain_total + gain_part
        bias_total = bias_total + bias_part
    shifted_grads = jnp.stack(grads_list)
    channel_ids = jnp.arange(CH, dtype=jnp.int32)
    forward_mask = jnp.any(channel_ids[None, :] == shift_fwd[:, None], axis=0)
    backward_mask = jnp.any(channel_ids[None, :] == shift_bwd[:, None], axis=0)
    later = jnp.concatenate([shifted_grads[:, 1:], jnp.zeros_like(shifted_grads[:, :1])], axis=1)
    earlier = jnp.concatenate([jnp.zeros_like(shifted_grads[:, :1]), shifted_grads[:, :-1]], axis=1)
    in_grad = jnp.where(forward_mask, later, jnp.where(backward_mask, earlier, shifted_grads))
    return (in_grad, weight_total * scale, gain_total * scale, bias_total * scale)
```

```python
import functools

import jax
import jax.numpy as jnp
from jax import lax
from jax.experimental import pallas as pl
from jax.experimental.pallas import tpu as pltpu
from jax.sharding import PartitionSpec as P

GROUP_CH = 20
epsilon = 1e-05
VMEM_BYTES = 48 * 1024 * 1024


F32 = jnp.float32
BF16 = jnp.bfloat16


def vmem_call(body, out_shape, n_in, scratch=(), smem=0, flops=0, nbytes=0, trans=0, name=None):
    specs = [pl.BlockSpec(memory_space=pltpu.SMEM)] * smem
    specs += [pl.BlockSpec(memory_space=pltpu.VMEM)] * (n_in - smem)
    many = isinstance(out_shape, (list, tuple))
    out_specs = [pl.BlockSpec(memory_space=pltpu.VMEM)] * len(out_shape) if many else pl.BlockSpec(memory_space=pltpu.VMEM)
    return pl.pallas_call(
        body,
        out_shape=out_shape,
        in_specs=specs,
        out_specs=out_specs,
        scratch_shapes=list(scratch),
        compiler_params=pltpu.CompilerParams(vmem_limit_bytes=VMEM_BYTES),
        cost_estimate=pl.CostEstimate(flops=flops, bytes_accessed=nbytes, transcendentals=trans),
        name=name,
    )


def shape(dims, dtype):
    return jax.ShapeDtypeStruct(dims, dtype)


def group_mean(sums, mean_mat):
    return jnp.dot(sums, mean_mat, preferred_element_type=F32, precision=lax.Precision.HIGHEST)


def column_of(plane, cols, lanes):
    return lax.broadcasted_iota(jnp.int32, (plane, lanes), 0) % cols


def transpose_body(perm_t, perm_c, own, other, g_t, g_c):
    rows = own.shape[0]
    for h, ref in enumerate((own, other)):
        g_t[:, h * rows:(h + 1) * rows] = lax.dot_general(
            perm_t[...], ref[...], (((1,), (1,)), ((), ())), preferred_element_type=F32
        ).astype(BF16)
        g_c[h * rows:(h + 1) * rows, :] = jnp.dot(
            ref[...], perm_c[...], preferred_element_type=F32
        ).astype(BF16)


def norm_body(frames, plane, cols, own, other, gain, bias, mean_mat, act_cat, center, inverse, sums):
    lanes = own.shape[1]
    total = 2 * frames

    def frame(f):
        ref = own if f < frames else other
        f = f % frames
        return ref[f * plane:(f + 1) * plane, :].astype(F32)

    for f in range(total):
        sums[f:f + 1, :] = jnp.sum(frame(f), axis=0, keepdims=True)
    center[...] = group_mean(sums[...], mean_mat[...])
    for f in range(total):
        sums[f:f + 1, :] = jnp.sum(jnp.square(frame(f) - center[f:f + 1, :]), axis=0, keepdims=True)
    inverse[...] = lax.rsqrt(group_mean(sums[...], mean_mat[...]) + epsilon)
    col = column_of(plane, cols, lanes)
    edge = jnp.zeros((cols, act_cat.shape[2]), BF16)
    for f in range(total):
        normed = (frame(f) - center[f:f + 1, :]) * inverse[f:f + 1, :]
        before = normed * gain[...] + bias[...]
        act = before / (1.0 + jnp.exp(-before))
        left = jnp.where(col > 0, pltpu.roll(act, 1, 0), 0.0)
        right = jnp.where(col < cols - 1, pltpu.roll(act, plane - 1, 0), 0.0)
        act_cat[f, 0:cols, :] = edge
        act_cat[f, cols + plane:, :] = edge
        act_cat[f, cols:cols + plane, :] = jnp.concatenate(
            [left.astype(BF16), act.astype(BF16), right.astype(BF16)], axis=1
        )


def kernel_grad_body(taps, plane, cols, g_t, act_cat, send, keep):
    total, _, width = act_cat.shape
    half = keep.shape[0]
    for i, a in enumerate(taps):
        view = act_cat[:, a * cols:a * cols + plane, :].reshape(total * plane, width)
        out = jnp.dot(g_t[...], view, preferred_element_type=F32)
        send[:, i * width:(i + 1) * width] = out[half:].astype(BF16)
        keep[:, i * width:(i + 1) * width] = out[:half]


def act_grad_body(
    frames, plane, cols, g_c, weight, own, other, gain, bias, mean_mat, center, inverse,
    shifted_grad, param_sums, grad_acc, sums_one, sums_two,
):
    lanes = own.shape[1]
    total = 2 * frames
    col = column_of(plane, cols, lanes)
    gap = jnp.zeros((cols, lanes), F32)
    rows = frames * plane
    for h in range(2):
        for b in range(3):
            for a in range(3):
                tap = 3 * a + b
                part = jnp.dot(
                    g_c[h * rows:(h + 1) * rows, :],
                    weight[:, tap * lanes:(tap + 1) * lanes],
                    preferred_element_type=F32,
                )
                for f in range(frames):
                    one = part[f * plane:(f + 1) * plane]
                    if a == 0:
                        one = jnp.concatenate([one[cols:], gap], axis=0)
                    if a == 2:
                        one = jnp.concatenate([gap, one[:plane - cols]], axis=0)
                    if b == 0:
                        one = jnp.where(col < cols - 1, pltpu.roll(one, plane - 1, 0), 0.0)
                    if b == 2:
                        one = jnp.where(col > 0, pltpu.roll(one, 1, 0), 0.0)
                    at = h * rows + f * plane
                    if a == 0 and b == 0:
                        grad_acc[at:at + plane, :] = one
                    else:
                        grad_acc[at:at + plane, :] += one

    def frame(f):
        ref = own if f < frames else other
        at = (f % frames) * plane
        return (ref[at:at + plane, :].astype(F32) - center[f:f + 1, :]) * inverse[f:f + 1, :]

    gain_sum = jnp.zeros((1, lanes), F32)
    bias_sum = jnp.zeros((1, lanes), F32)
    for f in range(total):
        normed = frame(f)
        before = normed * gain[...] + bias[...]
        sig = 1.0 / (1.0 + jnp.exp(-before))
        pre = grad_acc[f * plane:(f + 1) * plane, :] * sig * (1.0 + before * (1.0 - sig))
        pre_sum = jnp.sum(pre, axis=0, keepdims=True)
        pre_normed_sum = jnp.sum(pre * normed, axis=0, keepdims=True)
        gain_sum = gain_sum + pre_normed_sum
        bias_sum = bias_sum + pre_sum
        sums_one[f:f + 1, :] = pre_sum * gain[...]
        sums_two[f:f + 1, :] = pre_normed_sum * gain[...]
        grad_acc[f * plane:(f + 1) * plane, :] = pre * gain[...]
    param_sums[0:1, :] = gain_sum
    param_sums[1:2, :] = bias_sum
    sums_one[...] = group_mean(sums_one[...], mean_mat[...])
    sums_two[...] = group_mean(sums_two[...], mean_mat[...])
    for f in range(total):
        normed = frame(f)
        shifted_grad[f * plane:(f + 1) * plane, :] = (
            (grad_acc[f * plane:(f + 1) * plane, :] - sums_one[f:f + 1, :] - normed * sums_two[f:f + 1, :])
            * inverse[f:f + 1, :]
        ).astype(BF16)


def bit_reverse(values, bits):
    out = jnp.zeros_like(values)
    for i in range(bits):
        out = out | (((values >> i) & 1) << (bits - 1 - i))
    return out


def on_device(shifted, out_grad, conv_weight, norm_gain, norm_bias, shift_fwd, shift_bwd):
    count = lax.axis_size("frames")
    bits = count.bit_length() - 1
    chips = count // 2
    frames, row_count, cols, channels = shifted.shape[1:]
    plane = row_count * cols
    rows = frames * plane
    half = channels // 2
    own_rows = conv_weight.shape[0]
    me = lax.axis_index("frames")
    video = lax.axis_index("dp")
    core = me % 2
    chip = me // 2
    first_core = core == 0

    def swap(value, bit):
        return lax.ppermute(value, "frames", [(i, i ^ (1 << bit)) for i in range(count)])

    def swap_video(value):
        return lax.ppermute(value, "dp", [(0, 1), (1, 0)])

    split_weight = conv_weight.reshape(own_rows, 9, 2, half)
    low = split_weight[:, :, 0].reshape(own_rows, 9 * half)
    high = split_weight[:, :, 1].reshape(own_rows, 9 * half)
    weight_mine = jnp.where(first_core, low, high)
    weight_got = swap(jnp.where(first_core, high, low), 0)
    shard = jnp.where(
        first_core,
        jnp.concatenate([weight_mine, weight_got], axis=0),
        jnp.concatenate([weight_got, weight_mine], axis=0),
    )
    grad_own = out_grad.reshape(rows, channels)
    grad_other = swap(grad_own, 0)
    values = shifted.reshape(rows, channels)
    low, high = values[:, :half], values[:, half:]
    value_own = jnp.where(first_core, low, high)
    value_other = swap(jnp.where(first_core, high, low), 0)

    shards = {0: shard}
    for mask in sorted(range(1, chips), key=lambda m: (bin(m).count("1"), -m)):
        low_bit = (mask & -mask).bit_length() - 1
        shards[mask] = swap(shards[mask & (mask - 1)], low_bit + 1)
    weight = jnp.concatenate(
        [shards[m] for m in range(0, chips, 2)] + [shards[m] for m in range(1, chips, 2)], axis=0
    )

    ids = jnp.arange(channels, dtype=jnp.int32)
    relative = (ids // own_rows) ^ (chip * 2 + video)
    place = bit_reverse(relative, bits) * own_rows + ids % own_rows
    perm_t = (ids[:, None] == place[None, :]).astype(BF16)
    mask_of = (ids // (2 * own_rows)) ^ chip
    column = ((mask_of & 1) * (chips // 2) + (mask_of >> 1)) * (2 * own_rows) + ids % (2 * own_rows)
    perm_c = (column[:, None] == ids[None, :]).astype(BF16)
    channel_base = core * half
    gain = lax.dynamic_slice_in_dim(norm_gain, channel_base, half).reshape(1, half)
    bias = lax.dynamic_slice_in_dim(norm_bias, channel_base, half).reshape(1, half)
    group = jnp.arange(half, dtype=jnp.int32) // GROUP_CH
    mean_mat = (group[:, None] == group[None, :]).astype(F32) * (1.0 / (plane * GROUP_CH))

    g_t, g_c = vmem_call(
        transpose_body,
        [shape((channels, 2 * rows), BF16), shape((2 * rows, channels), BF16)],
        4,
        flops=8 * rows * channels * channels,
        nbytes=12 * rows * channels,
        name="transpose",
    )(perm_t, perm_c, grad_own, grad_other)
    act_cat, center, inverse = vmem_call(
        functools.partial(norm_body, frames, plane, cols),
        [
            shape((2 * frames, plane + 2 * cols, 3 * half), BF16),
            shape((2 * frames, half), F32),
            shape((2 * frames, half), F32),
        ],
        5,
        scratch=[pltpu.VMEM((2 * frames, half), F32)],
        flops=40 * rows * half,
        nbytes=20 * rows * half,
        trans=2 * rows * half,
        name="norm",
    )(value_own, value_other, gain, bias, mean_mat)

    finished = []
    for taps in ((0, 1), (2,)):
        width = 3 * half * len(taps)
        send, keep = vmem_call(
            functools.partial(kernel_grad_body, taps, plane, cols),
            [shape((channels // 2, width), BF16), shape((channels // 2, width), F32)],
            2,
            flops=4 * rows * channels * width,
            nbytes=4 * rows * (channels + width),
            name="kernel_grad",
        )(g_t, act_cat)
        for stage in range(bits):
            got = swap_video(send) if stage == 0 else swap(send, stage)
            summed = keep + got.astype(F32)
            left = summed.shape[0] // 2
            keep = summed[:left]
            if stage < bits - 1:
                send = summed[left:].astype(BF16)
            else:
                keep = summed
        finished.append(keep)
    scale = float(lax.axis_size("dp") * count * rows) ** (-0.5)
    block = jnp.concatenate(finished, axis=1) * scale
    block_got = swap_video(block.astype(BF16)).astype(F32)
    mine_is_own = core == video
    block_mine = jnp.where(mine_is_own, block, block_got)
    block_send = jnp.where(mine_is_own, block_got, block)
    block_pair = swap(block_send, 0)
    low = jnp.where(first_core, block_mine, block_pair).reshape(own_rows, 9, 1, half)
    high = jnp.where(first_core, block_pair, block_mine).reshape(own_rows, 9, 1, half)
    weight_grad = jnp.concatenate([low, high], axis=2).reshape(own_rows, 9 * channels)

    shifted_grad, param_sums = vmem_call(
        functools.partial(act_grad_body, frames, plane, cols),
        [shape((2 * rows, half), BF16), shape((2, half), F32)],
        9,
        scratch=[
            pltpu.VMEM((2 * rows, half), F32),
            pltpu.VMEM((2 * frames, half), F32),
            pltpu.VMEM((2 * frames, half), F32),
        ],
        flops=4 * rows * channels * 9 * half,
        nbytes=2 * channels * 9 * half + 8 * rows * channels,
        trans=2 * rows * half,
        name="act_grad",
    )(g_c, weight, value_own, value_other, gain, bias, mean_mat, center, inverse)

    sums = param_sums + swap_video(param_sums)
    for stage in range(1, bits):
        sums = sums + swap(sums, stage)
    sums_pair = swap(sums, 0)
    param_grads = jnp.where(
        first_core,
        jnp.concatenate([sums, sums_pair], axis=1),
        jnp.concatenate([sums_pair, sums], axis=1),
    ) * scale

    half_own, half_other = shifted_grad[:rows], shifted_grad[rows:]
    half_got = swap(half_other, 0)
    full = jnp.where(
        first_core,
        jnp.concatenate([half_own, half_got], axis=1),
        jnp.concatenate([half_got, half_own], axis=1),
    ).reshape(frames, plane, channels)
    forward_match = ids[None, :] == shift_fwd[:, None]
    backward_match = ids[None, :] == shift_bwd[:, None]
    forward_select = forward_match.astype(BF16)
    backward_select = backward_match.astype(BF16)
    forward_mask = jnp.any(forward_match, axis=0)
    backward_mask = jnp.any(backward_match, axis=0)
    contract_channels = (((1,), (1,)), ((), ()))
    rim_first = lax.dot_general(
        forward_select, full[0], contract_channels, preferred_element_type=F32
    ).astype(BF16)
    rim_last = lax.dot_general(
        backward_select, full[frames - 1], contract_channels, preferred_element_type=F32
    ).astype(BF16)
    up = [(i, i + 1) for i in range(count - 1)]
    before = lax.ppermute(rim_last, "frames", up)
    after = lax.ppermute(rim_first, "frames", [(j, i) for i, j in up])
    contract_fold = (((0,), (0,)), ((), ()))
    from_prev = lax.dot_general(
        before, backward_select, contract_fold, preferred_element_type=F32
    ).astype(BF16)
    from_next = lax.dot_general(
        after, forward_select, contract_fold, preferred_element_type=F32
    ).astype(BF16)
    later = jnp.concatenate([full[1:], from_next[None]], axis=0)
    earlier = jnp.concatenate([from_prev[None], full[:-1]], axis=0)
    in_grad = jnp.where(forward_mask, later, jnp.where(backward_mask, earlier, full))
    return (in_grad.reshape(shifted.shape), weight_grad, param_grads[0], param_grads[1])


def solution(mesh):
    split = P("dp", "frames", None, None, None)
    return jax.shard_map(
        on_device,
        mesh=mesh,
        in_specs=(split, split, P("frames", None), P(), P(), P(), P()),
        out_specs=(split, P("frames", None), P(), P()),
        check_vma=False,
    )
```
